32 devices in a mesh: region: 8 (over y, x, core), brick: 4 (over z).
Axes of the slice: x: 2, y: 2, z: 4, core: 2. Of those that a mesh axis runs over, the one named last changes fastest.
Arguments:
- velocity: float32 [3, 128, 64, 256], P(None, 'region', 'brick'), may hold values from -6 to 6
- viscosity: float32 [128, 64, 256], P('region', 'brick'), may hold values from 0.05 to 0.5
- marker_pos: float32 [3, 131072], P(None, ('region', 'brick')), as said below
- marker_force: float32 [3, 131072], P(None, ('region', 'brick')), may hold values from -240 to 240
- slot_lists: int32 [32, 8192], P(('region', 'brick')), may hold values from 0 to 16384, as said below
Outputs:
- predicted: float32 [3, 128, 64, 256], P(None, 'region', 'brick')
The draws below stay inside these ranges and needn't reach their ends.
Inputs may be any that keep to these rules, and one draw needn't show every extreme that they name: `slot_lists`: each row lists, in increasing order, the indices within its region group's 16384 markers of the markers whose second coordinate lies in that brick's rows, then is padded with 16384; every marker of the group stands in exactly one row, and in every region group one row is full. `marker_pos`: the first coordinate of a marker lies 2 or more cells inside its region group's slab, the third 2 or more cells from the grid's ends, and the second within the rows of the brick whose slot row lists it.
All inputs are finite; a program needn't handle non-finite values.
Results may differ from the reference program's by a relative error of at most 0.00088.
Values sent between devices are 32-bit elements; how exact they have to be, the bound alone decides.
No kernel may reach another device: no remote copies, remote signals or barrier semaphores. Data moves between devices by JAX's collectives and lax.ppermute only.
A program may use at most 192 MiB of HBM per device.

```python
import math
import jax
import jax.numpy as jnp
from jax import lax

CELL_X = 16
CELL_Y = 16
CELL_Z = 256
MARK_DEV = 4096
SLOTS = 8192
MARK_REG = 16384
MARKERS = 131072
GRID_X = 128
GRID_Y = 64
N_REGION = 8
N_BRICK = 4


def marker_layout(key):
    region_markers = MARK_DEV * N_BRICK
    centres = jax.random.randint(jax.random.fold_in(key, 11), (N_REGION,), 0, N_BRICK)
    counter = jnp.arange(region_markers, dtype=jnp.int32)
    others = jnp.mod(counter - SLOTS, N_BRICK - 1)
    keys = jax.random.split(jax.random.fold_in(key, 12), N_REGION)

    def one_region(centre, region_key):
        base = jnp.where(counter < SLOTS, centre, jnp.mod(centre + 1 + others, N_BRICK))
        return base[jax.random.permutation(region_key, region_markers)]
    return jax.vmap(one_region)(centres, keys).astype(jnp.int32)


def draw_slot_lists(key, part):
    assigned = marker_layout(key)
    region_markers = MARK_DEV * N_BRICK
    counter = jnp.arange(region_markers, dtype=jnp.int32)
    bricks_ids = jnp.arange(N_BRICK, dtype=jnp.int32)
    slot_ids = jnp.arange(SLOTS, dtype=jnp.int32)

    def rows_of(region_assign):
        order = jnp.argsort(region_assign * region_markers + counter).astype(jnp.int32)
        hits = (region_assign[None, :] == bricks_ids[:, None]).astype(jnp.int32).sum(axis=1)
        starts = jnp.cumsum(hits) - hits
        place = jnp.clip(starts[:, None] + slot_ids[None, :], 0, region_markers - 1)
        return jnp.where(slot_ids[None, :] < hits[:, None], order[place], region_markers)
    return jax.vmap(rows_of)(assigned).reshape(N_REGION * N_BRICK, SLOTS).astype(jnp.int32)


def draw_marker_pos(key, part):
    assigned = marker_layout(key).astype(jnp.float32)
    shape = assigned.shape
    first, second, third = jax.random.split(jax.random.fold_in(key, 23), 3)
    region = jnp.arange(N_REGION, dtype=jnp.float32)[:, None]
    coord_x = region * CELL_X + jax.random.uniform(first, shape, jnp.float32, 2.0, CELL_X - 2.0)
    coord_y = assigned * CELL_Y + jax.random.uniform(second, shape, jnp.float32, 0.0, 1.0 * CELL_Y)
    coord_z = jax.random.uniform(third, shape, jnp.float32, 2.0, CELL_Z - 2.0)
    return jnp.stack([coord_x, coord_y, coord_z]).reshape(3, N_REGION * MARK_DEV * N_BRICK).astype(jnp.float32)


def block_scale(own_key, shape, cuts, least, high):
    def one(dim, shards_of):
        steps = jax.random.uniform(jax.random.fold_in(jax.random.fold_in(own_key, 6), dim), (shards_of,), jnp.float32, least / len(cuts), high / len(cuts))
        return jnp.repeat(jnp.exp(steps), shape[dim] // shards_of).reshape((-1,) + (1,) * (len(shape) - dim - 1))

    gain = one(*cuts[0])
    for cut in cuts[1:]:
        gain = gain * one(*cut)
    return gain


def scatter_about(stream_key, dims, spread, bound, cuts=(), held_as=jnp.bfloat16):
    values = jax.random.normal(stream_key, dims, jnp.float32) * spread
    if len(cuts) > 0:
        values = block_scale(stream_key, dims, cuts, -0.22, 0.18) * values
    return jnp.clip(values, min=-bound, max=bound).astype(held_as)


def setup_inputs(seed: int = 0) -> dict:
    streams_of = jax.random.split(jax.random.key(seed), 6)
    return {
        "velocity": scatter_about(streams_of[0], (3, GRID_X, GRID_Y, CELL_Z), 1.0, 6.0, ((1, 8), (2, 4)), jnp.float32),
        "viscosity": jnp.clip(jnp.exp(math.log(0.5) - 2.3025851 * jax.random.uniform(streams_of[1], (GRID_X, GRID_Y, CELL_Z), jnp.float32) ** block_scale(streams_of[1], (GRID_X, GRID_Y, CELL_Z), ((0, 8), (1, 4)), -0.2, 0.2)), 0.05, 0.5),
        "marker_pos": draw_marker_pos(jax.random.fold_in(streams_of[5], 71), 0),
        "marker_force": scatter_about(streams_of[3], (3, MARKERS), 40.0, 240.0, ((1, 32),), jnp.float32),
        "slot_lists": draw_slot_lists(jax.random.fold_in(streams_of[5], 71), 0),
    }


def kernel_weight(dist):
    return jnp.where(jnp.abs(dist) < 2.0, 0.25 * (1.0 + jnp.cos(0.5 * jnp.pi * dist)), 0.0)


def spread_rows(pos, force, row_low, rows, col_low, cols, depth):
    x_centre = (col_low + jnp.arange(cols, dtype=jnp.int32)).astype(jnp.float32) + 0.5
    y_centre = (row_low + jnp.arange(rows, dtype=jnp.int32)).astype(jnp.float32) + 0.5
    z_centre = jnp.arange(depth, dtype=jnp.int32).astype(jnp.float32) + 0.5
    weight_x = kernel_weight(x_centre[:, None] - pos[0][None, :])
    weight_y = kernel_weight(y_centre[:, None] - pos[1][None, :])
    weight_z = kernel_weight(z_centre[None, :] - pos[2][:, None])
    factor = (force[:, None, None, :] * weight_x[None, :, None, :] * weight_y[None, None, :, :])
    factor = factor.reshape(3 * cols * rows, pos.shape[1]).astype(jnp.bfloat16)
    depth_low = weight_z.astype(jnp.bfloat16)
    factor, depth_low = lax.optimization_barrier((factor, depth_low))
    total = jnp.dot(factor.astype(jnp.float32), depth_low.astype(jnp.float32),
                    precision=lax.Precision.HIGHEST)
    return total.reshape(3, cols, rows, depth)


def side(array, axis, offset):
    parts = [slice(1, -1), slice(1, -1), slice(1, -1)]
    size = array.shape[array.ndim - 3 + axis]
    parts[axis] = slice(1 + offset, size - 1 + offset)
    if array.ndim == 4:
        return array[:, parts[0], parts[1], parts[2]]
    return array[parts[0], parts[1], parts[2]]


def advance(padded, force_field):
    vel = padded[:3]
    visc = padded[3]
    speed = side(vel, 0, 0)
    visc_mid = side(visc, 0, 0)
    diffusion = jnp.zeros_like(speed)
    advection = jnp.zeros_like(speed)
    for axis in range(3):
        upper = side(vel, axis, 1)
        lower = side(vel, axis, -1)
        visc_up = side(visc, axis, 1)
        visc_dn = side(visc, axis, -1)
        diffusion = diffusion + 0.5 * (visc_mid + visc_up) * (upper - speed) - 0.5 * (visc_mid + visc_dn) * (speed - lower)
        advection = advection + speed[axis][None] * (upper - lower) * 0.5
    return speed + 0.1 * (diffusion - advection + force_field)


def reference(velocity, viscosity, marker_pos, marker_force, slot_lists):
    groups = marker_pos.shape[1] // MARK_REG
    pos_all = marker_pos.reshape(3, groups, MARK_REG).transpose(1, 0, 2)
    force_all = marker_force.reshape(3, groups, MARK_REG).transpose(1, 0, 2)
    bricks_in = slot_lists.shape[0] // groups
    slots_all = slot_lists.reshape(groups, bricks_in, SLOTS)

    def region_field(items):
        region_pos, region_force, region_slots, region = items

        def brick_block(inner):
            listed, brick = inner
            valid = listed < MARK_REG
            safe = jnp.clip(listed, 0, MARK_REG - 1).astype(jnp.int32)
            pos = jnp.take(region_pos, safe, axis=1)
            force = jnp.take(region_force, safe, axis=1) * valid[None, :].astype(jnp.float32)
            return spread_rows(pos, force, brick * CELL_Y - 2, CELL_Y + 4, region * CELL_X, CELL_X, CELL_Z)

        blocks = lax.map(brick_block, (region_slots, jnp.arange(bricks_in, dtype=jnp.int32)))
        centre = blocks[:, :, :, 2:CELL_Y + 2, :]
        upper = blocks[:, :, :, CELL_Y + 2:, :]
        lower = blocks[:, :, :, :2, :]
        empty = jnp.zeros_like(upper[:1])
        from_below = jnp.concatenate([empty, upper[:-1]], axis=0)
        from_above = jnp.concatenate([lower[1:], empty], axis=0)
        centre = centre.at[:, :, :, :2, :].add(from_below)
        centre = centre.at[:, :, :, CELL_Y - 2:, :].add(from_above)
        return centre.transpose(1, 2, 0, 3, 4).reshape(3, CELL_X, bricks_in * CELL_Y, CELL_Z)

    fields = lax.map(region_field, (pos_all, force_all, slots_all, jnp.arange(groups, dtype=jnp.int32)))
    force_field = fields.transpose(1, 0, 2, 3, 4).reshape(velocity.shape)
    stacked = jnp.concatenate([velocity, viscosity[None]], axis=0)
    padded = jnp.pad(stacked, ((0, 0), (1, 1), (1, 1), (1, 1)))
    return advance(padded, force_field)
```

```python
import functools
import math

import jax
import jax.numpy as jnp
from jax import lax
from jax.experimental import pallas as pl
from jax.experimental.pallas import tpu as pltpu
from jax.sharding import PartitionSpec as P

LANES = 128
TILE = 2 * LANES
NQ = 24


def poly(t, coefs):
    out = jnp.full_like(t, coefs[-1])
    for c in coefs[-2::-1]:
        out = out * t + c
    return out


COS_COEFS = [(-1.0) ** n / math.factorial(2 * n) for n in range(8)]
SIN_COEFS = [(-1.0) ** n / math.factorial(2 * n + 1) for n in range(8)]


def window(u):
    shifted = u - 0.5
    cell = jnp.floor(shifted)
    angle = (0.5 * math.pi) * (shifted - cell)
    sq = angle * angle
    cosine = poly(sq, COS_COEFS)
    sine = angle * poly(sq, SIN_COEFS)
    first = cell - 1.0
    weights = (0.25 - 0.25 * sine, 0.25 + 0.25 * cosine, 0.25 + 0.25 * sine, 0.25 - 0.25 * cosine)
    residue = first - 4.0 * jnp.floor(first * 0.25)
    is_res = [residue == float(m) for m in range(4)]
    by_res = []
    for m in range(4):
        w = weights[3]
        for a in (2, 1, 0):
            w = jnp.where(is_res[(m - a) % 4], weights[a], w)
        by_res.append(w)
    return first, by_res


def prepare(mk_ref, prep_ref, groups, x_low, y_low):
    def part(q):
        return mk_ref[q * groups:(q + 1) * groups, :]

    def put(q, value):
        prep_ref[q * groups:(q + 1) * groups, :] = value

    z_first, z_w = window(part(2))
    block = jnp.floor(z_first * (1.0 / 16.0))
    put(0, block)
    put(1, z_first - 16.0 * block)
    for m in range(4):
        put(2 + m, z_w[m])
    y_first, y_w = window(part(1) - y_low)
    put(6, y_first)
    for m in range(4):
        put(7 + m, y_w[m])
    x_first, x_w = window(part(0) - x_low)
    put(11, x_first)
    for c in range(3):
        force = part(3 + c)
        for m in range(4):
            put(12 + 4 * c + m, force * x_w[m])


def add_tile(prep_ref, groups, tile, mxu, accs, cols, rows, depth):
    sub = lax.broadcasted_iota(jnp.int32, (8, LANES), 0)
    subf = sub.astype(jnp.float32)
    phase = sub & 3
    zero16 = jnp.zeros((16, LANES), jnp.bfloat16)

    def wide(q, g):
        return jnp.broadcast_to(prep_ref[pl.ds(q * groups + g, 1), :], (8, LANES))

    def pattern(q, g):
        w = wide(q + 3, g)
        for m in (2, 1, 0):
            w = jnp.where(phase == m, wide(q + m, g), w)
        return w

    def packed(a, b):
        return jnp.concatenate([a, b], axis=0).astype(jnp.bfloat16)

    halves = [2 * tile, 2 * tile + 1]
    zcols = []
    for g in halves:
        w = pattern(2, g)
        off = wide(1, g)
        zero = jnp.zeros_like(w)
        d0 = subf - off
        lo0 = jnp.where((d0 >= 0.0) & (d0 <= 3.0), w, zero)
        lo1 = jnp.where((d0 >= -8.0) & (d0 <= -5.0), w, zero)
        hi0 = jnp.where(d0 <= -13.0, w, zero)
        low = packed(lo0, lo1)
        high = packed(hi0, zero)
        blk = wide(0, g)
        blk16 = packed(blk, blk)
        prev = None
        col = []
        for t in range(depth // 16):
            here = blk16 == jnp.bfloat16(t)
            v = zero16 if prev is None else jnp.where(prev, high, zero16)
            col.append(jnp.where(here, low, v))
            prev = here
        zcols.append(jnp.concatenate(col, axis=0))
    pltpu.matmul_push_rhs(jnp.concatenate(zcols, axis=1), 0, mxu, transpose=True)

    wys = []
    xfirst = []
    for g in halves:
        w = pattern(7, g)
        zero = jnp.zeros_like(w)
        d0 = subf - wide(6, g)
        pair = []
        for h in range(rows // 8):
            d = d0 + 8.0 * h
            pair.append(jnp.where((d >= 0.0) & (d <= 3.0), w, zero))
        wys.append(pair)
        xf = wide(11, g)
        xfirst.append(packed(xf, xf))

    first = True
    for m in range(4):
        masks = {}
        for i in range(m, cols, 4):
            masks[i] = [
                (xf <= jnp.bfloat16(i)) & (xf >= jnp.bfloat16(i - 3)) for xf in xfirst
            ]
        for c in range(3):
            fx = [wide(12 + 4 * c + m, g) for g in halves]
            for rb in range(rows // 16):
                quad = [
                    packed(fx[n] * wys[n][2 * rb], fx[n] * wys[n][2 * rb + 1]) for n in range(2)
                ]
                for i in range(m, cols, 4):
                    lhs = jnp.concatenate(
                        [jnp.where(masks[i][n], quad[n], zero16) for n in range(2)], axis=1
                    )
                    pltpu.matmul_acc_lhs(
                        accs[(c * cols + i) * (rows // 16) + rb], lhs,
                        load_staged_rhs=0 if first else None,
                    )
                    first = False


def add_shard(mk_ref, prep_ref, accs, groups, x_low, y_low, cols, rows, depth):
    prepare(mk_ref, prep_ref, groups, x_low, y_low)

    def pair(t, carry):
        for mxu in range(2):
            add_tile(prep_ref, groups, 2 * t + mxu, mxu, accs[mxu], cols, rows, depth)
        return carry

    lax.fori_loop(0, groups // 4, pair, 0)


def corner(axes, cols, rows):
    region = lax.axis_index("region")
    brick = lax.axis_index("brick")
    return (region * cols).astype(jnp.float32), (brick * rows).astype(jnp.float32)


def pack_kernel(bricks, vel_ref, visc_ref, pos_ref, force_ref, mk_ref, s1_ref, s3_ref, xa_ref, xb_ref):
    cols, rows, depth = visc_ref.shape
    groups = pos_ref.shape[1] // LANES
    brick_odd = (lax.axis_index("brick") & 1) == 1
    region_odd = (lax.axis_index("region") & 1) == 1
    for c in range(3):
        for g in range(groups):
            lane = slice(g * LANES, (g + 1) * LANES)
            for src, q in ((pos_ref, c), (force_ref, 3 + c)):
                row = src[c:c + 1, lane]
                at = q * groups + g
                mk_ref[at:at + 1, :] = row
                s1_ref[at:at + 1, :] = row
                s3_ref[at:at + 1, :] = row

    def plane(c, i):
        return vel_ref[c, i] if c < 3 else visc_ref[i]

    base = 6 * groups
    for c in range(4):
        low, high = plane(c, 0), plane(c, cols - 1)
        xa_ref[c] = jnp.where(region_odd, low, high)
        xb_ref[c] = jnp.where(region_odd, high, low)
        for i in range(cols):
            p = plane(c, i)
            low, high = p[:1], p[rows - 1:rows]
            one = jnp.where(brick_odd, low, high)
            other = jnp.where(brick_odd, high, low)
            for h in range(depth // LANES):
                at = base + (h * 4 + c) * cols + i
                lane = slice(h * LANES, (h + 1) * LANES)
                s1_ref[at:at + 1, :] = one[:, lane]
                s3_ref[at:at + 1, :] = other[:, lane]


def pop(accs, index):
    return pltpu.matmul_pop(accs[0][index]) + pltpu.matmul_pop(accs[1][index])


def with_accumulators(kernel, naccs, depth, *refs):
    def run(*accs):
        kernel((accs[:naccs], accs[naccs:]), *refs)

    pl.run_scoped(
        run,
        *(pltpu.ACC(mxu)((16, depth), jnp.float32) for mxu in range(2) for _ in range(naccs)),
    )


def own_kernel(accs, vel_ref, visc_ref, mk_ref, base_ref, prep_ref):
    cols, rows, depth = visc_ref.shape
    groups = mk_ref.shape[0] // 6
    x_low, y_low = corner(None, cols, rows)
    add_shard(mk_ref, prep_ref, accs, groups, x_low, y_low, cols, rows, depth)
    lane = lax.broadcasted_iota(jnp.int32, (rows, depth), 1)
    row = lax.broadcasted_iota(jnp.int32, (rows, depth), 0)
    zero = jnp.zeros((rows, depth), jnp.float32)

    def around(p):
        jp = jnp.where(row == rows - 1, zero, pltpu.roll(p, rows - 1, 0))
        jm = jnp.where(row == 0, zero, pltpu.roll(p, 1, 0))
        kp = jnp.where(lane == depth - 1, zero, pltpu.roll(p, depth - 1, 1))
        km = jnp.where(lane == 0, zero, pltpu.roll(p, 1, 1))
        return jp, jm, kp, km

    for i in range(cols):
        mu = visc_ref[i]
        mu_ip = visc_ref[i + 1] if i + 1 < cols else zero
        mu_im = visc_ref[i - 1] if i > 0 else zero
        mu_all = (mu_ip, mu_im) + around(mu)
        v = [vel_ref[d, i] for d in range(3)]
        plus = [0.5 * ((mu + mu_all[2 * d]) - v[d]) for d in range(3)]
        minus = [0.5 * ((mu + mu_all[2 * d + 1]) + v[d]) for d in range(3)]
        total = 3.0 * mu
        for d in range(6):
            total = total + 0.5 * mu_all[d]
        for c in range(3):
            u = v[c]
            ip = vel_ref[c, i + 1] if i + 1 < cols else zero
            im = vel_ref[c, i - 1] if i > 0 else zero
            near = (ip, im) + around(u)
            sum_ = -(total * u)
            for d in range(3):
                sum_ = sum_ + plus[d] * near[2 * d] + minus[d] * near[2 * d + 1]
            base_ref[c, i] = u + 0.1 * (sum_ + pop(accs, c * cols + i))


def final_kernel(nfaces, accs, base_ref, s1_ref, s3_ref, xa_ref, xb_ref, ra_ref, rb_ref, *refs):
    *shards, out_ref, prep_ref = refs
    _, cols, rows, depth = base_ref.shape
    groups = (s1_ref.shape[0] - 8 * cols) // 6
    x_low, y_low = corner(None, cols, rows)
    for mk_ref in shards:
        add_shard(mk_ref, prep_ref, accs, groups, x_low, y_low, cols, rows, depth)

    region = lax.axis_index("region")
    regions = lax.axis_size("region")
    brick = lax.axis_index("brick")
    region_odd = (region & 1) == 1
    brick_odd = (brick & 1) == 1
    has_low = region > 0
    has_high = region < regions - 1

    for c in range(3):
        for i in range(cols):
            out_ref[c, i] = base_ref[c, i] + 0.1 * pop(accs, c * cols + i)

    def fix(sign, mu, mu_n, speed, u, u_n):
        along = speed if sign < 0 else -speed
        return 0.05 * ((mu + mu_n + along) * u_n - mu_n * u)

    zero = jnp.zeros((rows, depth), jnp.float32)
    own_high = [jnp.where(region_odd, xb_ref[c], xa_ref[c]) for c in range(4)]
    own_low = [jnp.where(region_odd, xa_ref[c], xb_ref[c]) for c in range(4)]
    far_high = [jnp.where(has_high, jnp.where(region_odd, rb_ref[c], ra_ref[c]), zero) for c in range(4)]
    far_low = [jnp.where(has_low, jnp.where(region_odd, ra_ref[c], rb_ref[c]), zero) for c in range(4)]
    for c in range(3):
        out_ref[c, cols - 1] += fix(1, own_high[3], far_high[3], own_high[0], own_high[c], far_high[c])
        out_ref[c, 0] += fix(-1, own_low[3], far_low[3], own_low[0], own_low[c], far_low[c])

    base = 6 * groups

    def face(ref, h, c):
        return ref[base + (h * 4 + c) * cols:base + (h * 4 + c + 1) * cols, :]

    none = jnp.zeros((cols, LANES), jnp.float32)
    for h in range(depth // LANES):
        lane = slice(h * LANES, (h + 1) * LANES)
        own_one = [face(s1_ref, h, c) for c in range(4)]
        own_two = [face(s3_ref, h, c) for c in range(4)]
        far_one = [face(shards[0], h, c) for c in range(4)] if nfaces else [none] * 4
        far_two = [none] * 4
        for t in range(1, nfaces):
            index = 2 ** (t + 1) - 2
            partner = brick ^ (index + 1)
            good = (partner - brick == 1) | (brick - partner == 1)
            far_two = [
                jnp.where(good, face(shards[index], h, c), far_two[c]) for c in range(4)
            ]
        high_own = [jnp.where(brick_odd, b, a) for a, b in zip(own_one, own_two)]
        low_own = [jnp.where(brick_odd, a, b) for a, b in zip(own_one, own_two)]
        high_far = [jnp.where(brick_odd, b, a) for a, b in zip(far_one, far_two)]
        low_far = [jnp.where(brick_odd, a, b) for a, b in zip(far_one, far_two)]
        for c in range(3):
            top = fix(1, high_own[3], high_far[3], high_own[1], high_own[c], high_far[c])
            low = fix(-1, low_own[3], low_far[3], low_own[1], low_own[c], low_far[c])
            for i in range(cols):
                out_ref[c, i, rows - 1:rows, lane] += top[i:i + 1]
                out_ref[c, i, 0:1, lane] += low[i:i + 1]


def body(velocity, viscosity, marker_pos, marker_force, slot_lists):
    del slot_lists
    cols, rows, depth = viscosity.shape
    bricks = lax.axis_size("brick")
    regions = lax.axis_size("region")
    groups = marker_pos.shape[1] // LANES
    f32 = jnp.float32
    vmem = pl.BlockSpec(memory_space=pltpu.VMEM)
    markers = jax.ShapeDtypeStruct((6 * groups, LANES), f32)
    with_face = jax.ShapeDtypeStruct((6 * groups + 8 * cols, LANES), f32)
    xface = jax.ShapeDtypeStruct((4, rows, depth), f32)
    mk, s1, s3, xa, xb = pl.pallas_call(
        functools.partial(pack_kernel, bricks),
        out_shape=(markers, with_face, with_face, xface, xface),
        in_specs=[vmem] * 4,
        out_specs=(vmem,) * 5,
        name="pack",
    )(velocity, viscosity, marker_pos, marker_force)

    partners = list(range(1, bricks))
    nfaces = 0
    received = {}
    for m in sorted(partners, key=lambda m: (m & (m + 1)) == 0):
        pairs = [(b, b ^ m) for b in range(bricks)]
        value = mk
        if m & (m + 1) == 0:
            value = s1 if m == 1 else s3
            nfaces += 1
        received[m] = lax.ppermute(value, "brick", pairs)
    ra = lax.ppermute(xa, "region", [(r, r ^ 1) for r in range(regions)])
    rb = lax.ppermute(
        xb, "region", [(r, (r + (1 if r % 2 else -1)) % regions) for r in range(regions)]
    )

    naccs = 3 * cols * rows // 16
    scratch = [pltpu.VMEM((NQ * groups, LANES), f32)]
    field = jax.ShapeDtypeStruct(velocity.shape, f32)
    base = pl.pallas_call(
        functools.partial(with_accumulators, own_kernel, naccs, depth),
        out_shape=field,
        in_specs=[vmem] * 3,
        out_specs=vmem,
        scratch_shapes=scratch,
        name="own",
    )(velocity, viscosity, mk)

    shards = [received[m] for m in partners]
    return pl.pallas_call(
        functools.partial(
            with_accumulators, functools.partial(final_kernel, nfaces), naccs, depth
        ),
        out_shape=field,
        in_specs=[vmem] * (7 + len(shards)),
        out_specs=vmem,
        scratch_shapes=scratch,
        name="final",
    )(base, s1, s3, xa, xb, ra, rb, *shards)


def solution(mesh):
    placed = (
        P(None, "region", "brick", None),
        P("region", "brick", None),
        P(None, ("region", "brick")),
        P(None, ("region", "brick")),
        P(("region", "brick"), None),
    )
    return jax.shard_map(
        body,
        mesh=mesh,
        in_specs=placed,
        out_specs=P(None, "region", "brick", None),
        check_vma=False,
    )
```

```python
import functools
import math

import jax
import jax.numpy as jnp
from jax import lax
from jax.experimental import pallas as pl
from jax.experimental.pallas import tpu as pltpu
from jax.sharding import PartitionSpec as P

LANES = 128
NQ = 24
GRANT = 16 << 20


def poly(t, coefs):
    out = jnp.full_like(t, coefs[-1])
    for c in coefs[-2::-1]:
        out = out * t + c
    return out


COS_COEFS = [(-1.0) ** n / math.factorial(2 * n) for n in range(8)]
SIN_COEFS = [(-1.0) ** n / math.factorial(2 * n + 1) for n in range(8)]


def window(u):
    shifted = u - 0.5
    cell = jnp.floor(shifted)
    angle = (0.5 * math.pi) * (shifted - cell)
    sq = angle * angle
    cosine = poly(sq, COS_COEFS)
    sine = angle * poly(sq, SIN_COEFS)
    first = cell - 1.0
    weights = (0.25 - 0.25 * sine, 0.25 + 0.25 * cosine, 0.25 + 0.25 * sine, 0.25 - 0.25 * cosine)
    residue = first - 4.0 * jnp.floor(first * 0.25)
    is_res = [residue == float(m) for m in range(4)]
    by_res = []
    for m in range(4):
        w = weights[3]
        for a in (2, 1, 0):
            w = jnp.where(is_res[(m - a) % 4], weights[a], w)
        by_res.append(w)
    return first, by_res


def prepare(mk_ref, prep_ref, at, groups, total, x_low, y_low):
    def part(q):
        return mk_ref[q * groups:(q + 1) * groups, :]

    def put(q, value):
        prep_ref[q * total + at:q * total + at + groups, :] = value

    z_first, z_w = window(part(2))
    block = jnp.floor(z_first * (1.0 / 16.0))
    put(0, block)
    put(1, z_first - 16.0 * block)
    for m in range(4):
        put(2 + m, z_w[m])
    y_first, y_w = window(part(1) - y_low)
    put(6, y_first)
    for m in range(4):
        put(7 + m, y_w[m])
    x_first, x_w = window(part(0) - x_low)
    put(11, x_first)
    for c in range(3):
        force = part(3 + c)
        for m in range(4):
            put(12 + 4 * c + m, force * x_w[m])


def spread(prep_ref, total, accs, cols, rows, depth, beside=None):
    sub = lax.broadcasted_iota(jnp.int32, (8, LANES), 0)
    subf = sub.astype(jnp.float32)
    phase = sub & 3
    zero16 = jnp.zeros((16, LANES), jnp.bfloat16)

    def wide(q, g):
        return jnp.broadcast_to(prep_ref[pl.ds(q * total + g, 1), :], (8, LANES))

    def pattern(q, g):
        w = wide(q + 3, g)
        for m in (2, 1, 0):
            w = jnp.where(phase == m, wide(q + m, g), w)
        return w

    def packed(a, b):
        return jnp.concatenate([a, b], axis=0).astype(jnp.bfloat16)

    def push(tile, mxu):
        zcols = []
        for g in (2 * tile, 2 * tile + 1):
            w = pattern(2, g)
            zero = jnp.zeros_like(w)
            d0 = subf - wide(1, g)
            lo0 = jnp.where((d0 >= 0.0) & (d0 <= 3.0), w, zero)
            lo1 = jnp.where((d0 >= -8.0) & (d0 <= -5.0), w, zero)
            hi0 = jnp.where(d0 <= -13.0, w, zero)
            low = packed(lo0, lo1)
            high = packed(hi0, zero)
            blk = wide(0, g)
            blk16 = packed(blk, blk)
            prev = None
            col = []
            for t in range(depth // 16):
                here = blk16 == jnp.bfloat16(t)
                v = zero16 if prev is None else jnp.where(prev, high, zero16)
                col.append(jnp.where(here, low, v))
                prev = here
            zcols.append(jnp.concatenate(col, axis=0))
        pltpu.matmul_push_rhs(jnp.concatenate(zcols, axis=1), 0, mxu, transpose=True)

    def stream(pair, following):
        wys, xfirst = [], []
        for mxu in range(2):
            tile = 2 * pair + mxu
            wys.append([])
            xfirst.append([])
            for g in (2 * tile, 2 * tile + 1):
                w = pattern(7, g)
                zero = jnp.zeros_like(w)
                d0 = subf - wide(6, g)
                halves = []
                for h in range(rows // 8):
                    d = d0 + 8.0 * h
                    halves.append(jnp.where((d >= 0.0) & (d <= 3.0), w, zero))
                wys[mxu].append(halves)
                xf = wide(11, g)
                xfirst[mxu].append(packed(xf, xf))
        first = True
        for m in range(4):
            inside = [
                {
                    i: [(xf <= jnp.bfloat16(i)) & (xf >= jnp.bfloat16(i - 3)) for xf in xfirst[mxu]]
                    for i in range(m, cols, 4)
                }
                for mxu in range(2)
            ]
            for c in range(3):
                for rb in range(rows // 16):
                    for mxu in range(2):
                        tile = 2 * pair + mxu
                        quad = []
                        for n in range(2):
                            f = wide(12 + 4 * c + m, 2 * tile + n)
                            wy = wys[mxu][n]
                            quad.append(packed(f * wy[2 * rb], f * wy[2 * rb + 1]))
                        for i in range(m, cols, 4):
                            lhs = jnp.concatenate(
                                [jnp.where(inside[mxu][i][n], quad[n], zero16) for n in range(2)],
                                axis=1,
                            )
                            pltpu.matmul_acc_lhs(
                                accs[mxu][(c * cols + i) * (rows // 16) + rb], lhs,
                                load_staged_rhs=0 if first and i == m else None,
                            )
                    if first and following is not None:
                        for mxu in range(2):
                            push(2 * following + mxu, mxu)
                    first = False

    pairs = total // 4
    for mxu in range(2):
        push(mxu, mxu)

    def step(t, carry):
        stream(t, t + 1)
        if beside is not None:
            beside(t)
        return carry

    lax.fori_loop(0, pairs - 1, step, 0)
    stream(pairs - 1, None)
    if beside is not None:
        beside(pairs - 1)


def corner(cols, rows):
    region = lax.axis_index("region")
    brick = lax.axis_index("brick")
    return (region * cols).astype(jnp.float32), (brick * rows).astype(jnp.float32)


def pack_kernel(vel_hbm, visc_hbm, pos_hbm, force_hbm, mk_ref, s1_ref, s3_ref, xa_ref, xb_ref,
                vel_ref, visc_ref, pos_ref, force_ref, sems):
    copies = [
        pltpu.make_async_copy(src, dst, sems.at[n])
        for n, (src, dst) in enumerate((
            (pos_hbm, pos_ref), (force_hbm, force_ref), (vel_hbm, vel_ref), (visc_hbm, visc_ref)
        ))
    ]
    for copy in copies:
        copy.start()
    cols, rows, depth = visc_ref.shape
    groups = pos_ref.shape[1] // LANES
    brick_odd = (lax.axis_index("brick") & 1) == 1
    region_odd = (lax.axis_index("region") & 1) == 1
    for first, copy, src in ((0, copies[0], pos_ref), (3, copies[1], force_ref)):
        copy.wait()
        for c in range(3):
            for g in range(groups):
                row = src[c:c + 1, g * LANES:(g + 1) * LANES]
                at = (first + c) * groups + g
                mk_ref[at:at + 1, :] = row
                s1_ref[at:at + 1, :] = row
                s3_ref[at:at + 1, :] = row
    copies[2].wait()
    copies[3].wait()

    def plane(c, i):
        return vel_ref[c, i] if c < 3 else visc_ref[i]

    base = 6 * groups
    for c in range(4):
        low, high = plane(c, 0), plane(c, cols - 1)
        xa_ref[c] = jnp.where(region_odd, low, high)
        xb_ref[c] = jnp.where(region_odd, high, low)
        for i in range(cols):
            low = vel_ref[c, i, 0:1, :] if c < 3 else visc_ref[i, 0:1, :]
            high = vel_ref[c, i, rows - 1:rows, :] if c < 3 else visc_ref[i, rows - 1:rows, :]
            one = jnp.where(brick_odd, low, high)
            other = jnp.where(brick_odd, high, low)
            for h in range(depth // LANES):
                at = base + (h * 4 + c) * cols + i
                lane = slice(h * LANES, (h + 1) * LANES)
                s1_ref[at:at + 1, :] = one[:, lane]
                s3_ref[at:at + 1, :] = other[:, lane]


def pop(accs, index):
    return pltpu.matmul_pop(accs[0][index]) + pltpu.matmul_pop(accs[1][index])


def with_accumulators(kernel, naccs, depth, *refs):
    def run(*accs):
        kernel((accs[:naccs], accs[naccs:]), *refs)

    pl.run_scoped(
        run,
        *(pltpu.ACC(mxu)((16, depth), jnp.float32) for mxu in range(2) for _ in range(naccs)),
    )


def own_kernel(accs, vel_ref, visc_ref, mk_ref, base_ref, prep_ref):
    cols, rows, depth = visc_ref.shape
    groups = mk_ref.shape[0] // 6
    x_low, y_low = corner(cols, rows)
    prepare(mk_ref, prep_ref, 0, groups, groups, x_low, y_low)
    lane = lax.broadcasted_iota(jnp.int32, (rows, depth), 1)
    at_low, at_high = lane == 0, lane == depth - 1
    zero = jnp.zeros((rows, depth), jnp.float32)

    def rolled(p):
        return (
            pltpu.roll(p, rows - 1, 0), pltpu.roll(p, 1, 0),
            pltpu.roll(p, depth - 1, 1), pltpu.roll(p, 1, 1),
        )

    def plane(i):
        up = jnp.minimum(i + 1, cols - 1)
        down = jnp.maximum(i - 1, 0)
        mu = 0.05 * visc_ref[i]
        v = [vel_ref[d, i] for d in range(3)]
        mu_n = (0.05 * visc_ref[up], 0.05 * visc_ref[down]) + rolled(mu)
        pairs = [mu + p for p in mu_n]
        pairs[4] = jnp.where(at_high, mu, pairs[4])
        pairs[5] = jnp.where(at_low, mu, pairs[5])
        centre = 1.0 - (((pairs[0] + pairs[1]) + (pairs[2] + pairs[3])) + (pairs[4] + pairs[5]))
        gain = []
        for d in range(3):
            along = 0.05 * v[d]
            gain += [pairs[2 * d] - along, pairs[2 * d + 1] + along]
        gain[4] = jnp.where(at_high, zero, gain[4])
        gain[5] = jnp.where(at_low, zero, gain[5])
        for c in range(3):
            near = (vel_ref[c, up], vel_ref[c, down]) + rolled(v[c])
            value = centre * v[c]
            for g, u in zip(gain, near):
                value = value + g * u
            base_ref[c, i] = value

    pairs = groups // 4
    each = -(-cols // pairs)

    def beside(t):
        for n in range(each):
            plane(jnp.minimum(each * t + n, cols - 1))

    spread(prep_ref, groups, accs, cols, rows, depth, beside)
    for c in range(3):
        for i in range(cols):
            base_ref[c, i] += 0.1 * pop(accs, c * cols + i)


def add_shards(shards, prep_ref, accs, groups, cols, rows, depth):
    x_low, y_low = corner(cols, rows)
    total = len(shards) * groups
    for n, mk_ref in enumerate(shards):
        prepare(mk_ref, prep_ref, n * groups, groups, total, x_low, y_low)
    spread(prep_ref, total, accs, cols, rows, depth)


def more_kernel(groups, accs, base_ref, *refs):
    *shards, out_ref, prep_ref = refs
    _, cols, rows, depth = base_ref.shape
    add_shards(shards, prep_ref, accs, groups, cols, rows, depth)
    for c in range(3):
        for i in range(cols):
            out_ref[c, i] = base_ref[c, i] + 0.1 * pop(accs, c * cols + i)


def final_kernel(groups, face_of, accs, base_ref, s1_ref, s3_ref, xa_ref, xb_ref, ra_ref, rb_ref, *refs):
    nfaces = len(face_of)
    faces, refs = refs[:nfaces], refs[nfaces:]
    *shards, out_hbm, out_ref, prep_ref, sems = refs
    _, cols, rows, depth = base_ref.shape
    add_shards(shards, prep_ref, accs, groups, cols, rows, depth)

    region = lax.axis_index("region")
    regions = lax.axis_size("region")
    brick = lax.axis_index("brick")
    region_odd = (region & 1) == 1
    brick_odd = (brick & 1) == 1
    has_low = region > 0
    has_high = region < regions - 1

    def fix(sign, own, d, c, far, taken):
        mu, u = own[3], own[c]
        along = mu - own[d] if sign > 0 else mu + own[d]
        return 0.05 * (
            along * (far[c] - taken[c]) + far[3] * (far[c] - u) - taken[3] * (taken[c] - u)
        )

    zero = jnp.zeros((rows, depth), jnp.float32)
    own_high = [jnp.where(region_odd, xb_ref[c], xa_ref[c]) for c in range(4)]
    own_low = [jnp.where(region_odd, xa_ref[c], xb_ref[c]) for c in range(4)]
    far_high = [jnp.where(has_high, jnp.where(region_odd, rb_ref[c], ra_ref[c]), zero) for c in range(4)]
    far_low = [jnp.where(has_low, jnp.where(region_odd, ra_ref[c], rb_ref[c]), zero) for c in range(4)]

    base = 6 * groups

    def face(ref, h, c):
        return ref[base + (h * 4 + c) * cols:base + (h * 4 + c + 1) * cols, :]

    none = jnp.zeros((cols, LANES), jnp.float32)
    top, low = {}, {}
    for h in range(depth // LANES):
        own_one = [face(s1_ref, h, c) for c in range(4)]
        own_two = [face(s3_ref, h, c) for c in range(4)]
        far_one, far_two = [none] * 4, [none] * 4
        for ref, m in zip(faces, face_of):
            got = [face(ref, h, c) for c in range(4)]
            if m == 1:
                far_one = got
            else:
                partner = brick ^ m
                good = (partner - brick == 1) | (brick - partner == 1)
                far_two = [jnp.where(good, g, f) for g, f in zip(got, far_two)]
        high_own = [jnp.where(brick_odd, b, a) for a, b in zip(own_one, own_two)]
        low_own = [jnp.where(brick_odd, a, b) for a, b in zip(own_one, own_two)]
        high_far = [jnp.where(brick_odd, b, a) for a, b in zip(far_one, far_two)]
        low_far = [jnp.where(brick_odd, a, b) for a, b in zip(far_one, far_two)]
        for c in range(3):
            top[c, h] = fix(1, high_own, 1, c, high_far, low_own)
            low[c, h] = fix(-1, low_own, 1, c, low_far, high_own)

    for c in range(3):
        for i in range(cols):
            value = base_ref[c, i] + 0.1 * pop(accs, c * cols + i)
            if i == 0:
                value = value + fix(-1, own_low, 0, c, far_low, own_low)
            if i == cols - 1:
                value = value + fix(1, own_high, 0, c, far_high, own_high)
            out_ref[c, i] = value
            for h in range(depth // LANES):
                lane = slice(h * LANES, (h + 1) * LANES)
                out_ref[c, i, rows - 1:rows, lane] += top[c, h][i:i + 1]
                out_ref[c, i, 0:1, lane] += low[c, h][i:i + 1]
        pltpu.make_async_copy(out_ref.at[c], out_hbm.at[c], sems.at[c]).start()
    for c in range(3):
        pltpu.make_async_copy(out_ref.at[c], out_hbm.at[c], sems.at[c]).wait()


def body(velocity, viscosity, marker_pos, marker_force, slot_lists):
    del slot_lists
    cols, rows, depth = viscosity.shape
    bricks = lax.axis_size("brick")
    regions = lax.axis_size("region")
    groups = marker_pos.shape[1] // LANES
    f32 = jnp.float32
    vmem = pl.BlockSpec(memory_space=pltpu.VMEM)
    hbm = pl.BlockSpec(memory_space=pltpu.HBM)
    params = pltpu.CompilerParams(vmem_limit_bytes=GRANT)
    markers = jax.ShapeDtypeStruct((6 * groups, LANES), f32)
    with_face = jax.ShapeDtypeStruct((6 * groups + 8 * cols, LANES), f32)
    xface = jax.ShapeDtypeStruct((4, rows, depth), f32)
    field = jax.ShapeDtypeStruct(velocity.shape, f32)
    mk, s1, s3, xa, xb = pl.pallas_call(
        pack_kernel,
        out_shape=(markers, with_face, with_face, xface, xface),
        in_specs=[hbm] * 4,
        out_specs=(vmem,) * 5,
        scratch_shapes=[
            pltpu.VMEM(x.shape, f32) for x in (velocity, viscosity, marker_pos, marker_force)
        ] + [pltpu.SemaphoreType.DMA((4,))],
        compiler_params=params,
        name="pack",
    )(*(
        pltpu.with_memory_space_constraint(x, pltpu.HBM)
        for x in (velocity, viscosity, marker_pos, marker_force)
    ))

    partners = list(range(1, bricks))
    face_of = [m for m in partners if m & (m + 1) == 0]
    received = {}
    for m in sorted(partners, key=lambda m: m in face_of):
        value = mk if m not in face_of else s1 if m == 1 else s3
        received[m] = lax.ppermute(value, "brick", [(b, b ^ m) for b in range(bricks)])
    ra = lax.ppermute(xa, "region", [(r, r ^ 1) for r in range(regions)])
    rb = lax.ppermute(
        xb, "region", [(r, (r + (1 if r % 2 else -1)) % regions) for r in range(regions)]
    )

    naccs = 3 * cols * rows // 16

    def prep(shards):
        return pltpu.VMEM((NQ * groups * shards, LANES), f32)

    base = pl.pallas_call(
        functools.partial(with_accumulators, own_kernel, naccs, depth),
        out_shape=field,
        in_specs=[vmem] * 3,
        out_specs=vmem,
        scratch_shapes=[prep(1)],
        compiler_params=params,
        name="own",
    )(velocity, viscosity, mk)

    early, late = partners[:1], partners[1:]
    if late:
        base = pl.pallas_call(
            functools.partial(
                with_accumulators, functools.partial(more_kernel, groups), naccs, depth
            ),
            out_shape=field,
            in_specs=[vmem] * (1 + len(early)),
            out_specs=vmem,
            scratch_shapes=[prep(len(early))],
            compiler_params=params,
            name="more",
        )(base, *(received[m] for m in early))
    else:
        late = early
    return pl.pallas_call(
        functools.partial(
            with_accumulators, functools.partial(final_kernel, groups, face_of), naccs, depth
        ),
        out_shape=field,
        in_specs=[vmem] * (7 + len(face_of) + len(late)),
        out_specs=hbm,
        scratch_shapes=[
            pltpu.VMEM(velocity.shape, f32), prep(len(late)), pltpu.SemaphoreType.DMA((3,))
        ],
        compiler_params=params,
        name="final",
    )(base, s1, s3, xa, xb, ra, rb, *(received[m] for m in face_of), *(received[m] for m in late))


def solution(mesh):
    placed = (
        P(None, "region", "brick", None),
        P("region", "brick", None),
        P(None, ("region", "brick")),
        P(None, ("region", "brick")),
        P(("region", "brick"), None),
    )
    return jax.shard_map(
        body,
        mesh=mesh,
        in_specs=placed,
        out_specs=P(None, "region", "brick", None),
        check_vma=False,
    )
```
